32 devices in a mesh: groups: 2 (over y), tm: 4 (over z), space: 2 (over x), chan: 2 (over core).
Axes of the slice: x: 2, y: 2, z: 4, core: 2. Of those that a mesh axis runs over, the one named last changes fastest.
Arguments:
- latents: bfloat16 [8, 8, 160, 384], P(('groups', 'tm'), 'space', None, 'chan'), parts along dimension 0, may hold values from -30 to 30
- norm_gain: float32 [384], P('chan'), may hold values from 0.1 to 1.9
- conv_weight: bfloat16 [3, 3, 3, 384, 384], P(None, None, None, 'chan'), may hold values from -0.0625 to 0.0625
- conv_bias: float32 [384], P('chan'), may hold values from -2 to 2
- attention_gain: float32 [384], P('chan'), may hold values from 0.1 to 1.9
- qkv_weight: bfloat16 [384, 1152], P('chan'), may hold values from -3 to 3
- out_weight: bfloat16 [384, 384], replicated, may hold values from -0.3125 to 0.3125
Outputs:
- block_output: bfloat16 [8, 8, 160, 384], P(('groups', 'tm'), 'space', None, 'chan'), parts along dimension 0
The draws below stay inside these ranges and needn't reach their ends.
There are 2 independent parts, one for each index of `groups`. The reference program is written for one: setup_inputs(seed, part) draws one part's arguments, and reference() takes and returns one part's arrays. A program takes and returns all parts, laid end to end along the dimension named above; an argument that names none is the same for every part. Nothing has to cross between parts.
All inputs are finite; a program needn't handle non-finite values.
Results may differ from the reference program's by a relative error of at most 0.019.
Values may be sent and summed in bfloat16 or wider, within the bound.
No kernel may reach another device: no remote copies, remote signals or barrier semaphores. Data moves between devices by JAX's collectives and lax.ppermute only.
A program may use at most 64 MiB of HBM per device.

```python
import math
import jax
import jax.numpy as jnp
from jax import lax

CHANNELS = 384
FRAME_W = 160
FRAMES = 4
HEIGHT = 8
FRAME_POS = 1280


def draw_latents(key, part):
    subkeys = jax.random.split(key, 3)
    array_shape = (FRAMES, HEIGHT, FRAME_W, CHANNELS)
    channel_ramp = jnp.exp(math.log(3.0) * (jnp.arange(CHANNELS, dtype=jnp.float32) / (CHANNELS - 1) - 0.5))
    jitter = jnp.exp(jax.random.uniform(subkeys[0], (CHANNELS,), jnp.float32, -0.35, 0.35))
    entries = jnp.clip(jax.random.normal(subkeys[1], array_shape, jnp.float32), -4.0, 4.0)
    row_scale = jnp.exp(jax.random.uniform(subkeys[2], (FRAMES, HEIGHT, FRAME_W, 1), jnp.float32, math.log(0.3), math.log(3.0)))
    return (entries * row_scale * (channel_ramp * jitter)).astype(jnp.bfloat16)


def draw_qkv_weight(key, part):
    subkeys = jax.random.split(key, 1)
    entries = jnp.clip(jax.random.normal(subkeys[0], (CHANNELS, 3 * CHANNELS), jnp.float32), -4.0, 4.0) / math.sqrt(CHANNELS)
    return entries.astype(jnp.bfloat16)


def block_levels(own_key, dims, shards, least, high):
    level, own = 1.0, jax.random.fold_in(own_key, 6)
    for dim, blocks in shards:
        steps = jnp.exp(jax.random.uniform(jax.random.fold_in(own, dim), (blocks,), jnp.float32, least / len(shards), high / len(shards)))
        level = level * jnp.repeat(steps, dims[dim] // blocks).reshape([-1 if axis == dim else 1 for axis in range(len(dims))])
    return level


def noise(stream_key, extent, width, reach, cuts=(), held_as=jnp.bfloat16):
    result = width * jax.random.normal(stream_key, extent, jnp.float32)
    if cuts:
        result = result * block_levels(stream_key, extent, cuts, -0.22, 0.18)
    return jnp.clip(result, -reach, reach).astype(held_as)


def setup_inputs(seed: int = 0, part: int = 0) -> dict:
    key_list = jax.random.split(jax.random.key(seed), 8)
    own_keys = jax.random.split(jax.random.fold_in(key_list[7], part), 8)
    latents = draw_latents(jax.random.fold_in(jax.random.fold_in(key_list[7], part), 71), part)
    norm_gain = jnp.clip(1.0 + 0.18 * jax.random.normal(key_list[1], (CHANNELS,), jnp.float32), 0.1, 1.9)
    conv_weight = noise(key_list[2], (3, 3, 3, CHANNELS, CHANNELS), (27 * CHANNELS) ** -0.5, 0.0625, ((3, 2),))
    conv_bias = noise(key_list[3], (CHANNELS,), 0.5, 2.0, ((0, 2),), jnp.float32)
    attention_gain = jnp.clip(1.0 + 0.18 * jax.random.normal(key_list[4], (CHANNELS,), jnp.float32), 0.1, 1.9)
    qkv_weight = draw_qkv_weight(jax.random.fold_in(key_list[7], 71), part)
    out_weight = noise(key_list[6], (CHANNELS, CHANNELS), CHANNELS ** -0.5, 0.3125)
    return dict(latents=latents, norm_gain=norm_gain, conv_weight=conv_weight, conv_bias=conv_bias, attention_gain=attention_gain, qkv_weight=qkv_weight, out_weight=out_weight)


epsilon = 1e-06

def normalize(values, gain):
    mean_square = lax.optimization_barrier(jnp.mean(values * values, axis=-1, keepdims=True))
    return values * lax.rsqrt(mean_square + epsilon) * gain

def reference(latents, norm_gain, conv_weight, conv_bias, attention_gain, qkv_weight, out_weight):
    as_float = latents.astype(jnp.float32)
    first = jax.nn.silu(normalize(as_float, norm_gain)).astype(jnp.bfloat16)
    padded = jnp.pad(first, ((2, 0), (1, 1), (1, 1), (0, 0)))
    zero_index = jnp.zeros((), jnp.int32)

    def frame_conv(frame_index):
        window = lax.dynamic_slice(padded, (frame_index, zero_index, zero_index, zero_index), (3, HEIGHT + 2, FRAME_W + 2, CHANNELS))
        total = jnp.zeros((HEIGHT * FRAME_W, CHANNELS), jnp.float32)
        for frame_off in range(3):
            for row_off in range(3):
                for col_off in range(3):
                    patch = window[frame_off, row_off:row_off + HEIGHT, col_off:col_off + FRAME_W].reshape(HEIGHT * FRAME_W, CHANNELS)
                    total = total + jnp.dot(patch, conv_weight[frame_off, row_off, col_off], preferred_element_type=jnp.float32)
        return total
    conv = lax.map(frame_conv, jnp.arange(FRAMES, dtype=jnp.int32))
    stream = (as_float.reshape(FRAMES, FRAME_POS, CHANNELS) + conv + conv_bias).astype(jnp.bfloat16)
    stream_float = stream.astype(jnp.float32)
    second = normalize(stream_float, attention_gain).astype(jnp.bfloat16)
    score_scale = 1.0 / math.sqrt(CHANNELS)

    def frame_attention(inputs):
        qkv = jnp.dot(inputs, qkv_weight, preferred_element_type=jnp.float32).astype(jnp.bfloat16)
        queries = qkv[:, :CHANNELS]
        key_rows = qkv[:, CHANNELS:2 * CHANNELS]
        value_rows = qkv[:, 2 * CHANNELS:]
        scores = lax.dot_general(queries, key_rows, (((1,), (1,)), ((), ())), preferred_element_type=jnp.float32) * score_scale
        peak = lax.optimization_barrier(jnp.max(scores, axis=1, keepdims=True))
        weights = jnp.exp(scores - peak)
        total = lax.optimization_barrier(jnp.sum(weights, axis=1, keepdims=True))
        attended = (jnp.dot(weights.astype(jnp.bfloat16), value_rows, preferred_element_type=jnp.float32) / total).astype(jnp.bfloat16)
        return jnp.dot(attended, out_weight, preferred_element_type=jnp.float32).astype(jnp.bfloat16)
    projected = lax.map(frame_attention, second)
    output = (stream_float + projected.astype(jnp.float32)).astype(jnp.bfloat16)
    return output.reshape(FRAMES, HEIGHT, FRAME_W, CHANNELS)
```

```python
import functools
import math

import jax
import jax.numpy as jnp
from jax import lax
from jax.experimental import pallas as pl
from jax.experimental.pallas import tpu as pltpu
from jax.sharding import PartitionSpec as P

epsilon = 1e-06
F32 = jnp.float32
BF16 = jnp.bfloat16
PAIR = [(0, 1), (1, 0)]


def swapped(value, axis="chan"):
    return lax.ppermute(value, axis, PAIR)


def passed_along(shard, axis, by):
    peers = lax.axis_size(axis)
    pairs = [(i, i + by) for i in range(peers) if 0 <= i + by < peers]
    return lax.ppermute(shard, axis, pairs)


def next_span(shard):
    peers = lax.axis_size("tm")
    return lax.ppermute(shard, "tm", [(i, (i + 1) % peers) for i in range(peers)])


def second_next_span(shard):
    last = lax.axis_size("tm") - 1
    pairs = []
    for core in range(2):
        pairs.append((core, 1 - core))
        if last == 1:
            pairs.append((2 + core, 3 - core))
        for span in range(1, last):
            pairs.append((2 * span + core, 2 * span + 2 + core))
        if last > 1:
            pairs.append((2 * last + core, 2 + core))
    return lax.ppermute(shard, ("tm", "chan"), pairs)


def matmul(a, b):
    return jnp.dot(a, b, preferred_element_type=F32)


def scores_of(queries, keys):
    return lax.dot_general(queries, keys, (((1,), (1,)), ((), ())), preferred_element_type=F32)


def call(kernel, outs, args, scratch=(), flops=0, aliases=None, limit=None, source=pltpu.VMEM):
    shapes = tuple(jax.ShapeDtypeStruct(shape, dtype) for shape, dtype in outs)
    read = sum(math.prod(arg.shape) * arg.dtype.itemsize for arg in args)
    if source == pltpu.HBM:
        args = [pltpu.with_memory_space_constraint(arg, pltpu.HBM) for arg in args]
    params = {"vmem_limit_bytes": limit or 16 << 20}
    return pl.pallas_call(
        kernel,
        out_shape=shapes,
        in_specs=[pl.BlockSpec(memory_space=source)] * len(args),
        out_specs=tuple(pl.BlockSpec(memory_space=pltpu.VMEM) for _ in outs),
        scratch_shapes=list(scratch),
        input_output_aliases=aliases or {},
        compiler_params=pltpu.CompilerParams(**params),
        cost_estimate=pl.CostEstimate(flops=flops, bytes_accessed=read, transcendentals=0),
    )(*args)


def load_kernel(own_hbm, gain_hbm, scaled_ref, sums_ref, own_ref, gain_ref, own_sem, gain_sem):
    copies = (
        pltpu.make_async_copy(own_hbm, own_ref, own_sem),
        pltpu.make_async_copy(gain_hbm, gain_ref, gain_sem),
    )
    for copy in copies:
        copy.start()
    for copy in copies:
        copy.wait()
    own = own_ref[...].astype(F32)
    scaled_ref[...] = own * gain_ref[...]
    sums_ref[...] = jnp.sum(own * own, axis=1, keepdims=True)


def first_kernel(channels, scaled_ref, sums_ref, other_ref, out_ref):
    other = other_ref[...].astype(F32)
    sums = sums_ref[...] + jnp.sum(other * other, axis=1, keepdims=True)
    value = scaled_ref[...] * lax.rsqrt(sums / channels + epsilon)
    out_ref[...] = (value / (1.0 + jnp.exp(-value))).astype(BF16)


def fetch_kernel(source_ref, out_ref, sem):
    copy = pltpu.make_async_copy(source_ref, out_ref, sem)
    copy.start()
    copy.wait()


def prep_kernel(
    channels,
    scale,
    weight_ref,
    weight_other_ref,
    out_weight_ref,
    bias_ref,
    bias_other_ref,
    gain_ref,
    gain_other_ref,
    own_ref,
    other_ref,
    query_key_ref,
    value_out_ref,
    vectors_out_ref,
    natural_ref,
    full_ref,
):
    core = lax.axis_index("chan")
    half = weight_ref.shape[0]
    full_ref[pl.ds(pl.multiple_of(core * half, half), half), :] = weight_ref[...]
    full_ref[pl.ds(pl.multiple_of((1 - core) * half, half), half), :] = weight_other_ref[...]
    query_key_ref[...] = (
        scores_of(full_ref[:, :channels], full_ref[:, channels : 2 * channels]) * scale
    ).astype(BF16)
    value_out = lax.dot_general(
        out_weight_ref[...],
        full_ref[:, 2 * channels :],
        (((0,), (1,)), ((), ())),
        preferred_element_type=F32,
    ).astype(BF16)
    low, high = value_out[:half, :], value_out[half:, :]
    value_out_ref[:half, :] = jnp.where(core == 0, high, low)
    value_out_ref[half:, :] = jnp.where(core == 0, low, high)

    def laid(own, other):
        return jnp.concatenate(
            [jnp.where(core == 0, own, other), jnp.where(core == 0, other, own)], axis=1
        )

    vectors_out_ref[:1, :] = laid(bias_ref[...], bias_other_ref[...])
    vectors_out_ref[1:, :] = laid(gain_ref[...], gain_other_ref[...])
    natural_ref[...] = laid(own_ref[...].astype(F32), other_ref[...].astype(F32)).astype(BF16)


def shifted(cells, width, dest_ref):
    rows, chan = cells.shape
    wide = cells.astype(F32)
    column = lax.rem(lax.broadcasted_iota(jnp.int32, (rows, 1), 0), width)
    left = jnp.where(column == 0, 0.0, pltpu.roll(wide, 1, 0))
    right = jnp.where(column == width - 1, 0.0, pltpu.roll(wide, rows - 1, 0))
    dest_ref[:, :chan] = left.astype(BF16)
    dest_ref[:, chan : 2 * chan] = cells
    dest_ref[:, 2 * chan :] = right.astype(BF16)


def windows(width, rows):
    if lax.axis_size("space") == 2:
        place = lax.axis_index("space")
        inner = [(pl.multiple_of(place * width, width), rows - width)]
        edge = [(pl.multiple_of((1 - place) * (rows - width), width), width)]
        return inner, edge
    return [(width, rows - 2 * width)], [(0, width), (rows - width, width)]


def joined(ref, parts):
    values = [ref[pl.ds(start, size), :] for start, size in parts]
    return values[0] if len(values) == 1 else jnp.concatenate(values, axis=0)


def rim_products(width, halo_refs, rim_ref, weight_ref):
    if len(halo_refs) == 1:
        shifted(halo_refs[0][...], width, rim_ref)
        return [matmul(rim_ref[...], weight_ref[(1 - lax.axis_index("space")) * 2])]
    products = []
    for halo_ref, row_off in zip(halo_refs, (0, 2)):
        shifted(halo_ref[...], width, rim_ref)
        products.append(matmul(rim_ref[...], weight_ref[row_off]))
    return products


def add_rim(width, halo_refs, rim_ref, weight_ref, acc_ref):
    _, edge = windows(width, acc_ref.shape[0])
    products = rim_products(width, halo_refs, rim_ref, weight_ref)
    for (start, size), product in zip(edge, products):
        acc_ref[pl.ds(start, size), :] += product


def add_inner(width, cells_ref, laid_ref, weight_ref, acc_ref, before):
    rows = acc_ref.shape[0]
    shifted(cells_ref[...], width, laid_ref)
    middle = matmul(laid_ref[...], weight_ref[1])
    acc_ref[...] = middle if before is None else before[...] + middle
    acc_ref[width:, :] += matmul(laid_ref[: rows - width, :], weight_ref[0])
    acc_ref[: rows - width, :] += matmul(laid_ref[width:, :], weight_ref[2])


def finish(total, natural, bias, rounded_ref, kept_ref):
    rounded_ref[...] = total.astype(BF16)
    kept_ref[...] = total + natural.astype(F32) + bias


def chained(width, frame_off, halo_refs, cells_ref, taps_ref, before_ref, acc_ref, laid, rim):
    span = lax.axis_index("tm")
    back = 2 - frame_off

    @pl.when(span >= back)
    def _():
        add_inner(width, cells_ref, laid, taps_ref.at[frame_off], acc_ref, before_ref)

    @pl.when(span < back)
    def _():
        acc_ref[...] = before_ref[...]

    @pl.when(span >= back - 1)
    def _():
        add_rim(width, halo_refs, rim, taps_ref.at[frame_off + 1], acc_ref)


def conv_a_kernel(width, cells_ref, taps_ref, acc_ref, laid_ref):
    add_inner(width, cells_ref, laid_ref, taps_ref.at[2], acc_ref, None)


def conv_b_kernel(width, halo_count, *refs):
    cells_ref, taps_ref, before_ref, acc_ref, laid_ref, rim_ref = refs[halo_count:]
    chained(
        width, 1, refs[:halo_count], cells_ref, taps_ref, before_ref, acc_ref, laid_ref, rim_ref
    )


def conv_c_kernel(width, halo_count, *refs):
    cells_ref, taps_ref, before_ref, natural_ref, vectors_ref = refs[halo_count : halo_count + 5]
    acc_ref, rounded_ref, kept_ref, laid_ref, rim_ref = refs[halo_count + 5 :]
    chained(
        width, 0, refs[:halo_count], cells_ref, taps_ref, before_ref, acc_ref, laid_ref, rim_ref
    )
    inner, _ = windows(width, acc_ref.shape[0])
    finish(
        joined(acc_ref, inner), joined(natural_ref, inner), vectors_ref[:1, :], rounded_ref, kept_ref
    )


def conv_end_kernel(width, halo_count, *refs):
    taps_ref, acc_ref, natural_ref, vectors_ref, rounded_ref, kept_ref, rim_ref = refs[halo_count:]
    _, edge = windows(width, acc_ref.shape[0])
    kept_ref[...] = joined(acc_ref, edge)

    @pl.when(lax.axis_index("tm") >= 2)
    def _():
        products = rim_products(width, refs[:halo_count], rim_ref, taps_ref.at[0])
        for index, product in enumerate(products):
            kept_ref[index * width : (index + 1) * width, :] += product

    finish(kept_ref[...], joined(natural_ref, edge), vectors_ref[:1, :], rounded_ref, kept_ref)


def stream_kernel(channels, kept_ref, got_ref, vectors_ref, stream_ref, second_ref, keys_ref):
    stream = (kept_ref[...] + got_ref[...].astype(F32)).astype(BF16)
    stream_ref[...] = stream
    value = stream.astype(F32)
    sums = jnp.sum(value * value, axis=1, keepdims=True)
    second_ref[...] = (
        value * lax.rsqrt(sums / channels + epsilon) * vectors_ref[1:, :]
    ).astype(BF16)
    count = keys_ref.shape[0]
    core = lax.axis_index("chan")
    keys_ref[...] = second_ref[pl.ds(pl.multiple_of(core * count, 16), count), :]


def near_kernel(
    second_inner_ref,
    second_edge_ref,
    keys_inner_ref,
    keys_edge_ref,
    query_key_ref,
    stream_inner_ref,
    stream_edge_ref,
    queries_ref,
    peak_ref,
    total_ref,
    summed_ref,
    own_ref,
    keys_ref,
):
    core = lax.axis_index("chan")
    half = own_ref.shape[1]
    inner = second_inner_ref.shape[0]
    keys_ref[: keys_inner_ref.shape[0], :] = keys_inner_ref[...]
    keys_ref[keys_inner_ref.shape[0] :, :] = keys_edge_ref[...]
    queries_ref[:inner, :] = matmul(second_inner_ref[...], query_key_ref[...]).astype(BF16)
    queries_ref[inner:, :] = matmul(second_edge_ref[...], query_key_ref[...]).astype(BF16)
    scores = scores_of(keys_ref[...], queries_ref[...])
    peak = jnp.max(scores, axis=0, keepdims=True)
    weights = jnp.exp(scores - peak)
    peak_ref[...] = peak
    total_ref[...] = jnp.sum(weights, axis=0, keepdims=True)
    summed_ref[...] = weighted(keys_ref[...], weights)
    for rows, stream_ref in ((slice(0, inner), stream_inner_ref), (slice(inner, None), stream_edge_ref)):
        stream = stream_ref[...].astype(F32)
        own_ref[rows, :] = jnp.where(core == 0, stream[:, :half], stream[:, half:]).astype(BF16)


def weighted(keys, weights):
    return lax.dot_general(
        keys, weights.astype(BF16), (((0,), (0,)), ((), ())), preferred_element_type=F32
    )


def attended(queries, keys, before, total, summed):
    scores = scores_of(keys, queries)
    peak = jnp.maximum(before, jnp.max(scores, axis=0, keepdims=True))
    weights = jnp.exp(scores - peak)
    shrink = jnp.exp(before - peak)
    total = total * shrink + jnp.sum(weights, axis=0, keepdims=True)
    return peak, total, summed * shrink + weighted(keys, weights)


def far_kernel(
    queries_ref,
    keys_ref,
    peak_ref,
    total_ref,
    summed_ref,
    peak_out_ref,
    total_out_ref,
    summed_out_ref,
):
    peak_out_ref[...], total_out_ref[...], summed_out_ref[...] = attended(
        queries_ref[...], keys_ref[...], peak_ref[...], total_ref[...], summed_ref[...]
    )


def far_end_kernel(
    start,
    queries_ref,
    keys_ref,
    peak_ref,
    total_ref,
    summed_ref,
    value_out_ref,
    sent_ref,
    kept_ref,
    log_ref,
):
    half, count = kept_ref.shape
    window = slice(start, start + count)
    peak, total, summed = attended(
        queries_ref[window, :],
        keys_ref[...],
        peak_ref[:, window],
        total_ref[:, window],
        summed_ref[:, window],
    )
    mixed = (summed * (1.0 / total)).astype(BF16)
    log_total = peak + jnp.log(total)
    log_ref[...] = log_total
    projected = matmul(value_out_ref[...], mixed)
    sent_ref[:half, :] = projected[:half, :].astype(BF16)
    kept_ref[...] = projected[half:, :]
    top = log_total.astype(BF16).astype(F32)
    rest = log_total - top
    middle = rest.astype(BF16).astype(F32)
    low = rest - middle
    spare = sent_ref.shape[0] - half
    row = lax.broadcasted_iota(jnp.int32, (spare, count), 0)
    pieces = jnp.where(row == 0, top, jnp.where(row == 1, middle, low))
    sent_ref[half:, :] = pieces.astype(BF16)


def combined(kept_ref, log_ref, got_ref, own):
    half = kept_ref.shape[0]
    pieces = got_ref[half:, :].astype(F32)
    other_log = pieces[:1, :] + pieces[1:2, :] + pieces[2:3, :]
    share = 1.0 / (1.0 + jnp.exp(other_log - log_ref[...]))
    projected = share * kept_ref[...] + (1.0 - share) * got_ref[:half, :].astype(F32)
    projected = jnp.transpose(projected).astype(BF16).astype(F32)
    return (own.astype(F32) + projected).astype(BF16)


def final_a_kernel(kept_ref, log_ref, got_ref, own_ref, out_ref):
    out_ref[...] = combined(kept_ref, log_ref, got_ref, own_ref[: out_ref.shape[0], :])


def final_b_kernel(width, kept_ref, log_ref, got_ref, own_ref, begun_ref, out_ref):
    begun = begun_ref.shape[0]
    output = combined(kept_ref, log_ref, got_ref, own_ref[begun:, :])
    inner, edge = windows(width, out_ref.shape[0])
    row = 0
    for start, size in inner + edge:
        done = min(max(begun - row, 0), size)
        if done:
            out_ref[pl.ds(start, done), :] = begun_ref[row : row + done, :]
        if done < size:
            rest = slice(row + done - begun, row + size - begun)
            out_ref[pl.ds(start + done, size - done), :] = output[rest, :]
        row += size


def far_rows(keys):
    if lax.axis_size("space") == 2:
        return swapped(keys, "space")
    rows = lax.all_gather(keys, "space", axis=0, tiled=True)
    count = keys.shape[0]
    return jnp.roll(rows, -lax.axis_index("space") * count, axis=0)[count:]


def rim_rows(cells, width):
    count = lax.axis_size("space")
    head, tail = cells[:width], cells[-width:]
    if count == 2:
        place = lax.axis_index("space")
        return [swapped(jnp.where(place == 0, tail, head), "space")]
    return [passed_along(tail, "space", 1), passed_along(head, "space", -1)]


def block(latents, norm_gain, conv_weight, conv_bias, attention_gain, qkv_weight, out_weight):
    _, row_count, width, half = latents.shape
    channels = conv_weight.shape[4]
    pos_count = row_count * width
    scale = 1.0 / math.sqrt(channels)
    taps = conv_weight.reshape(3, 3, 3 * half, channels)
    own = latents.reshape(pos_count, half)
    other = swapped(own)
    scaled, sums = call(
        load_kernel,
        [((pos_count, half), F32), ((pos_count, 1), F32)],
        [own, norm_gain[None]],
        scratch=[
            pltpu.VMEM((pos_count, half), BF16),
            pltpu.VMEM((1, half), F32),
            pltpu.SemaphoreType.DMA,
            pltpu.SemaphoreType.DMA,
        ],
        source=pltpu.HBM,
    )
    (first,) = call(
        functools.partial(first_kernel, channels),
        [((pos_count, half), BF16)],
        [scaled, sums, other],
    )
    previous = next_span(first)
    earlier = second_next_span(previous)
    rims_a = rim_rows(first, width)
    rims_b = rim_rows(previous, width)
    rims_c = rim_rows(earlier, width)
    weight_other = swapped(qkv_weight)
    bias, gain = conv_bias[None], attention_gain[None]
    bias_other = swapped(bias)
    gain_other = swapped(gain)
    (taps,) = call(
        fetch_kernel,
        [(taps.shape, BF16)],
        [taps],
        scratch=[pltpu.SemaphoreType.DMA],
        source=pltpu.HBM,
    )
    query_key, value_out, vectors, natural = call(
        functools.partial(prep_kernel, channels, scale),
        [
            ((channels, channels), BF16),
            ((channels, channels), BF16),
            ((2, channels), F32),
            ((pos_count, channels), BF16),
        ],
        [qkv_weight, weight_other, out_weight, bias, bias_other, gain, gain_other, own, other],
        scratch=[pltpu.VMEM((channels, 3 * channels), BF16)],
        flops=4 * channels**3,
    )
    acc_shape = ((pos_count, channels), F32)
    laid = pltpu.VMEM((pos_count, 3 * half), BF16)
    rim = pltpu.VMEM((width, 3 * half), BF16)
    flops = 2 * 8 * half * channels * pos_count
    count = len(rims_a)
    (acc,) = call(
        functools.partial(conv_a_kernel, width),
        [acc_shape],
        [first, taps],
        scratch=[laid],
        flops=flops,
    )
    (acc,) = call(
        functools.partial(conv_b_kernel, width, count),
        [acc_shape],
        [*rims_a, previous, taps, acc],
        scratch=[laid, rim],
        flops=flops,
        aliases={count + 2: 0},
    )
    edge_count = count * width
    inner_count = pos_count - edge_count
    acc, rounded_inner, kept_inner = call(
        functools.partial(conv_c_kernel, width, count),
        [acc_shape, ((inner_count, channels), BF16), ((inner_count, channels), F32)],
        [*rims_b, earlier, taps, acc, natural, vectors],
        scratch=[laid, rim],
        flops=flops,
        aliases={count + 2: 0},
    )
    rounded_edge, kept_edge = call(
        functools.partial(conv_end_kernel, width, count),
        [((edge_count, channels), BF16), ((edge_count, channels), F32)],
        [*rims_c, taps, acc, natural, vectors],
        scratch=[rim],
        flops=flops // 8,
    )
    parts = []
    for rounded, kept in ((rounded_inner, kept_inner), (rounded_edge, kept_edge)):
        rows = rounded.shape[0]
        got = swapped(rounded)
        stream, second, keys = call(
            functools.partial(stream_kernel, channels),
            [((rows, channels), BF16), ((rows, channels), BF16), ((rows // 2, channels), BF16)],
            [kept, got, vectors],
        )
        parts.append((stream, second, keys, far_rows(keys)))
    (stream_inner, second_inner, keys_inner, far_inner) = parts[0]
    (stream_edge, second_edge, keys_edge, far_edge) = parts[1]
    key_count = pos_count // 2
    column = ((1, pos_count), F32)
    sums_shape = ((channels, pos_count), F32)
    queries, peak, total, summed, own_stream = call(
        near_kernel,
        [((pos_count, channels), BF16), column, column, sums_shape, ((pos_count, half), BF16)],
        [second_inner, second_edge, keys_inner, keys_edge, query_key, stream_inner, stream_edge],
        scratch=[pltpu.VMEM((key_count, channels), BF16)],
        flops=2 * pos_count * channels * (channels + 2 * key_count),
    )
    peak, total, summed = call(
        far_kernel,
        [column, column, sums_shape],
        [queries, far_inner, peak, total, summed],
        flops=4 * pos_count * channels * far_inner.shape[0],
    )
    begun = -(-pos_count // 256) * 128
    pieces = []
    for start, size in ((0, begun), (begun, pos_count - begun)):
        sent, projected, log_total = call(
            functools.partial(far_end_kernel, start),
            [((half + 16, size), BF16), ((half, size), F32), ((1, size), F32)],
            [queries, far_edge, peak, total, summed, value_out],
            flops=2 * size * channels * (channels + 2 * far_edge.shape[0]),
        )
        pieces.append([projected, log_total, swapped(sent), own_stream])
    (output,) = call(final_a_kernel, [((begun, half), BF16)], pieces[0])
    (output,) = call(
        functools.partial(final_b_kernel, width), [((pos_count, half), BF16)], [*pieces[1], output]
    )
    return output.reshape(1, row_count, width, half)


def solution(mesh):
    placed = (
        P(("groups", "tm"), "space", None, "chan"),
        P("chan"),
        P(None, None, None, "chan", None),
        P("chan"),
        P("chan"),
        P("chan", None),
        P(),
    )
    return jax.shard_map(
        block,
        mesh=mesh,
        in_specs=placed,
        out_specs=P(("groups", "tm"), "space", None, "chan"),
        check_vma=False,
    )
```
